32 devices in a mesh: dp: 16 (over z, y, x), blk: 2 (over core).
Axes of the slice: x: 2, y: 2, z: 4, core: 2. Of those that a mesh axis runs over, the one named last changes fastest.
Arguments:
- vectors: float32 [16384, 96], P('dp'), may hold values from -16 to 16
- codes: int32 [16384, 8], P('dp'), may hold values from 0 to 255, as said below
- weights: bfloat16 [16384], P('dp'), may hold values from 0.25 to 4
- ridge: float32 [1], replicated, may hold values from 0.1 to 0.5
Outputs:
- codebooks: float32 [8, 256, 96], replicated
- residual: float32 [16384, 96], P('dp')
- distortion: float32 [], replicated
The draws below stay inside these ranges and needn't reach their ends.
Inputs may be any that keep to these rules, and one draw needn't show every extreme that they name: `codes`: 8 codebook indices per vector.
All inputs are finite; a program needn't handle non-finite values.
Results may differ from the reference program's by a relative error of at most 0.0003.
Values sent between devices are 32-bit elements; how exact they have to be, the bound alone decides.
A program may use at most 128 MiB of HBM per device.

```python
import math
import jax
import jax.numpy as jnp
from jax import lax

D = 96
K = 256
M = 8
ITERS = 8
ROWS = 16384


def shared_codes(key):
    base = jax.random.fold_in(key, 11)
    keys = jax.random.split(base, 4)
    perms = jax.vmap(lambda single: jax.random.permutation(single, K))(jax.random.split(keys[0], M))
    perms = perms.astype(jnp.int32)
    first = jax.random.randint(keys[1], (ROWS, M), 0, K).astype(jnp.int32)
    second = jax.random.randint(keys[2], (ROWS, M), 0, K).astype(jnp.int32)
    ranks = jnp.minimum(first, second)
    tied = jax.random.randint(keys[3], (ROWS, 1), 0, 2).astype(jnp.int32)
    ranks = jnp.where(tied == 1, ranks[:, :1], ranks).astype(jnp.int32)
    return perms[jnp.arange(M)[None, :], ranks].astype(jnp.int32)


def draw_codes(key, part):
    return shared_codes(key)


def draw_vectors(key, part):
    codes = shared_codes(key)
    keys = jax.random.split(jax.random.fold_in(key, 23), 2)
    truth = 0.5 * jax.random.truncated_normal(keys[0], -3.0, 3.0, (M, K, D), jnp.float32)
    recon = jnp.zeros((ROWS, D), jnp.float32)
    for book in range(M):
        recon = recon + jnp.take(truth[book], codes[:, book], axis=0)
    position = jnp.arange(ROWS, dtype=jnp.float32) / ROWS
    level = (0.3 * (1.0 + 2.0 * position))[:, None]
    noise = jax.random.truncated_normal(keys[1], -4.0, 4.0, (ROWS, D), jnp.float32)
    return recon + level * noise


def steps_of(own_key, dims, cuts, least, high):
    factor_of = 1.0
    for dim, shards_of in cuts:
        steps = jax.random.uniform(jax.random.fold_in(jax.random.fold_in(own_key, 6), dim), (shards_of,), jnp.float32, least / len(cuts), high / len(cuts))
        factor_of = factor_of * jnp.repeat(jnp.exp(steps), dims[dim] // shards_of).reshape((-1,) + (1,) * (len(dims) - 1 - dim))
    return factor_of


def setup_inputs(seed: int = 0) -> dict:
    arg_keys = jax.random.split(jax.random.key(seed), 5)
    vectors = draw_vectors(jax.random.fold_in(arg_keys[4], 71), 0)
    codes = draw_codes(jax.random.fold_in(arg_keys[4], 71), 0)
    weights = jnp.clip(jnp.exp(math.log(4.0) - 2.7725887 * jax.random.uniform(arg_keys[2], (ROWS,), jnp.float32) ** steps_of(arg_keys[2], (ROWS,), ((0, 16),), -0.2, 0.2)), 0.25, 4.0).astype(jnp.bfloat16)
    ridge = jnp.clip(jnp.exp(jax.random.uniform(arg_keys[3], (1,), jnp.float32, math.log(0.1), math.log(0.5))), 0.1, 0.5)
    return {"vectors": vectors, "codes": codes, "weights": weights, "ridge": ridge}


HIGH = lax.Precision.HIGHEST


def reference(vectors, codes, weights, ridge):
    rows = vectors.shape[0]
    mass = weights.astype(jnp.float32)
    weighted = vectors * mass[:, None]
    count_list = []
    sum_list = []
    for book in range(M):
        count_list.append(jax.ops.segment_sum(mass, codes[:, book], num_segments=K))
        sum_list.append(jax.ops.segment_sum(weighted, codes[:, book], num_segments=K))
    counts = jnp.stack(count_list)
    right = jnp.stack(sum_list).reshape(M * K, D)
    blocks = []
    for first in range(M):
        row_blocks = []
        for second in range(M):
            if first == second:
                row_blocks.append(jnp.diag(counts[first]))
            else:
                joint = codes[:, first] * K + codes[:, second]
                row_blocks.append(jax.ops.segment_sum(mass, joint, num_segments=K * K).reshape(K, K))
        blocks.append(jnp.concatenate(row_blocks, axis=1))
    gram = jnp.concatenate(blocks, axis=0)
    total_mass = jnp.sum(counts[0])
    lam = ridge[0] * total_mass / K
    precond = (counts + lam).reshape(M * K, 1)
    solution = jnp.zeros((M * K, D), jnp.float32)
    remain = right
    scaled = remain / precond
    direction = scaled
    inner = jnp.sum(remain * scaled, axis=0)
    for step in range(ITERS):
        image = jnp.dot(gram, direction, precision=HIGH) + lam * direction
        alpha = inner / jnp.sum(direction * image, axis=0)
        solution = solution + alpha * direction
        remain = remain - alpha * image
        scaled = remain / precond
        fresh = jnp.sum(remain * scaled, axis=0)
        direction = scaled + (fresh / inner) * direction
        inner = fresh
    codebooks = solution.reshape(M, K, D)
    recon = jnp.zeros_like(vectors)
    for book in range(M):
        recon = recon + jnp.take(codebooks[book], codes[:, book], axis=0)
    residual = vectors - recon
    distortion = jnp.sum(mass[:, None] * residual * residual) / (total_mass * D)
    return codebooks, residual, distortion
```

```python
import functools

import jax
import jax.numpy as jnp
from jax import lax
from jax.experimental import pallas as pl
from jax.experimental.pallas import tpu as pltpu
from jax.sharding import PartitionSpec as P

K = 256
M = 8
ITERS = 8
MESH = pl.DeviceIdType.MESH
HIGH = lax.Precision.HIGHEST
F32 = jnp.float32
BF16 = jnp.bfloat16
NT = (((1,), (1,)), ((), ()))


def vmem():
    return pl.BlockSpec(memory_space=pltpu.VMEM)


def anywhere():
    return pl.BlockSpec(memory_space=pl.ANY)


def split2(value):
    high = value.astype(BF16)
    low = (value - high.astype(F32)).astype(BF16)
    return high, low


def split3(value):
    high = value.astype(BF16)
    rest = value - high.astype(F32)
    middle = rest.astype(BF16)
    low = (rest - middle.astype(F32)).astype(BF16)
    return high, middle, low


def column_groups(groups, width):
    best = 1
    for count in range(1, groups + 1):
        if groups % count == 0 and width % count == 0 and (width // count) % 8 == 0:
            best = count
    return best


def hot_t(row, levels):
    return jnp.where(levels == row, jnp.ones((), BF16), jnp.zeros((), BF16))


def partial_kernel(ncg, nblk, codes_ref, weights_ref, vectors_ref, part_ref):
    rows, width = vectors_ref.shape
    cols = width // ncg
    blk = lax.axis_index("blk")
    parts = jnp.concatenate(split3(vectors_ref[...].T), axis=0)
    levels = lax.broadcasted_iota(jnp.int32, (K, rows), 0).astype(F32).astype(BF16)
    mass = weights_ref[...].astype(BF16)
    for member in range(M // nblk):
        row = codes_ref[pl.ds(nblk * member + blk, 1), :].astype(F32).astype(BF16)
        hot = jnp.where(levels == row, jnp.broadcast_to(mass, (K, rows)), jnp.zeros((), BF16))
        sums = lax.dot_general(parts, hot, NT, preferred_element_type=F32)
        total = sums[:width] + sums[width : 2 * width] + sums[2 * width :]
        for group in range(ncg):
            part_ref[group, member] = total[group * cols : (group + 1) * cols]


def exchange_kernel(n, ncg, gsz, codes_ref, weights_ref, part_ref, codes_out, weights_out, right_out, send_sem, recv_sem, own_sem):
    me = lax.axis_index("dp")
    barrier = pltpu.get_barrier_semaphore()

    def greet(k, carry):
        pl.semaphore_signal(barrier, inc=1, device_id={"dp": lax.rem(me + k, n)}, device_id_type=MESH)
        return carry

    lax.fori_loop(1, n, greet, 0)
    my_part = part_ref.at[lax.rem(me // gsz, ncg), lax.rem(me, gsz)]
    own = [
        pltpu.make_async_copy(codes_ref, codes_out.at[me], own_sem.at[0]),
        pltpu.make_async_copy(weights_ref, weights_out.at[me], own_sem.at[1]),
        pltpu.make_async_copy(my_part, right_out.at[me], own_sem.at[2]),
    ]
    for copy in own:
        copy.start()
    pl.semaphore_wait(barrier, n - 1)

    def copies(k):
        to = lax.rem(me + k, n)
        piece = part_ref.at[lax.rem(to // gsz, ncg), lax.rem(to, gsz)]
        pairs = [(codes_ref, codes_out.at[me]), (weights_ref, weights_out.at[me]), (piece, right_out.at[me])]
        return [
            pltpu.make_async_remote_copy(
                src_ref=source,
                dst_ref=target,
                send_sem=send_sem.at[i, k],
                recv_sem=recv_sem.at[i, k],
                device_id={"dp": to},
                device_id_type=MESH,
            )
            for i, (source, target) in enumerate(pairs)
        ]

    def start(k, carry):
        for copy in copies(k):
            copy.start()
        return carry

    def finish(k, carry):
        for copy in copies(k):
            copy.wait()
        return carry

    lax.fori_loop(1, n, start, 0)
    for copy in own:
        copy.wait()
    lax.fori_loop(1, n, finish, 0)


def gram_kernel(nblk, gsz, codes_ref, weights_ref, gram_ref, count_ref, total_ref):
    step = pl.program_id(0)
    rows = codes_ref.shape[2]
    book = nblk * lax.rem(lax.axis_index("dp"), gsz) + lax.axis_index("blk")

    @pl.when(step == 0)
    def _():
        total_ref[...] = jnp.zeros_like(total_ref)

    levels = lax.broadcasted_iota(jnp.int32, (K, rows), 0).astype(F32).astype(BF16)
    mass = weights_ref[0].astype(BF16)
    mine = codes_ref[0, pl.ds(book, 1), :].astype(F32).astype(BF16)
    weighted = jnp.where(levels == mine, jnp.broadcast_to(mass, (K, rows)), jnp.zeros((), BF16))
    for other in range(M):
        row = codes_ref[0, other : other + 1, :].astype(F32).astype(BF16)
        block = pl.ds(other * K, K)
        total_ref[block, :] += lax.dot_general(hot_t(row, levels), weighted, NT, preferred_element_type=F32)

    @pl.when(step == pl.num_programs(0) - 1)
    def _():
        ones = jnp.ones((8, K), F32)
        for other in range(M):
            block = pl.ds(other * K, K)
            value = total_ref[block, :]
            high, low = split2(value)
            gram_ref[block, :K] = high
            gram_ref[block, K:] = low
            count_ref[other] = lax.dot_general(ones, value, NT, precision=HIGH, preferred_element_type=F32)


def solve_kernel(n, nblk, ncg, gsz, ridge_ref, gram_ref, count_ref, pieces_ref, out_ref,
                 swap, solution, remain, direction, inverse, send_sem, recv_sem, far_send, far_recv, near_send, near_recv):
    cols = pieces_ref.shape[1]
    dp = lax.axis_index("dp")
    blk = lax.axis_index("blk")
    group, member = dp // gsz, lax.rem(dp, gsz)
    book = nblk * member + blk
    bases = (group // ncg) * ncg
    mine = lax.rem(group, ncg)
    half = M // nblk

    def team(k):
        to = lax.rem(book + k, M)
        return {"dp": group * gsz + to // nblk, "blk": lax.rem(to, nblk)}

    def far(k):
        return {"dp": (bases + lax.rem(mine + k, ncg)) * gsz + member, "blk": blk}

    barrier = pltpu.get_barrier_semaphore()
    for k in range(1, M):
        pl.semaphore_signal(barrier, inc=1, device_id=team(k), device_id_type=MESH)
    for k in range(1, ncg):
        pl.semaphore_signal(barrier, inc=1, device_id=far(k), device_id_type=MESH)

    def add(s, total):
        return total + pieces_ref[s]

    right = lax.fori_loop(1, n, add, pieces_ref[0])
    lam = ridge_ref[0] * (jnp.sum(count_ref[0, 0:1, :]) / K)
    for q in range(M):
        inverse[q] = 1.0 / (count_ref[q] + lam)
    pl.semaphore_wait(barrier, M - 1 + ncg - 1)

    def share(slot, value):
        swap[slot, book] = value
        copies = [
            pltpu.make_async_remote_copy(
                src_ref=swap.at[slot, book],
                dst_ref=swap.at[slot, book],
                send_sem=send_sem.at[slot, k],
                recv_sem=recv_sem.at[slot, k],
                device_id=team(k),
                device_id_type=MESH,
            )
            for k in range(1, M)
        ]
        for copy in copies:
            copy.start()
        for copy in copies:
            copy.wait()

    def column(pieces):
        total = pieces[0]
        for piece in pieces[1:]:
            total = total + piece
        return jnp.sum(total, axis=1, keepdims=True)

    share(0, right)
    pieces = []
    for q in range(M):
        r = swap[0, q]
        z = r * inverse[q, 0:1, :]
        remain[q] = r
        direction[q] = z
        solution[q] = jnp.zeros_like(r)
        pieces.append(r * z)

    def iterate(step, inner):
        slot = lax.rem(step + 1, 2)
        product = None
        for q in range(M):
            left = jnp.concatenate(split2(direction[q]), axis=0)
            term = jnp.dot(left, gram_ref[pl.ds(q * K, K), :], preferred_element_type=F32)
            product = term if product is None else product + term
        image = (product[:cols, :K] + product[cols:, :K]) + (product[:cols, K:] + product[cols:, K:])
        share(slot, image)
        pieces = []
        for q in range(M):
            d = direction[q]
            pieces.append(d * (swap[slot, q] + lam * d))
        alpha = inner / column(pieces)
        pieces = []
        for q in range(M):
            d = direction[q]
            r = remain[q] - alpha * (swap[slot, q] + lam * d)
            solution[q] = solution[q] + alpha * d
            remain[q] = r
            pieces.append(r * (r * inverse[q, 0:1, :]))
        fresh = column(pieces)
        beta = fresh / inner
        for q in range(M):
            direction[q] = remain[q] * inverse[q, 0:1, :] + beta * direction[q]
        return fresh

    lax.fori_loop(0, ITERS, iterate, column(pieces))

    for q in range(M):
        out_ref[mine, q] = solution[q]
    part = pl.ds(blk * half, half)
    away = [
        pltpu.make_async_remote_copy(
            src_ref=solution.at[part],
            dst_ref=out_ref.at[mine, part],
            send_sem=far_send.at[k],
            recv_sem=far_recv.at[k],
            device_id=far(k),
            device_id_type=MESH,
        )
        for k in range(1, ncg)
    ]
    for copy in away:
        copy.start()
    relays = []
    for k in range(1, ncg):
        away[k - 1].wait_recv()
        source = lax.rem(mine - k + ncg, ncg)
        for other in range(1, nblk):
            relay = pltpu.make_async_remote_copy(
                src_ref=out_ref.at[source, part],
                dst_ref=out_ref.at[source, part],
                send_sem=near_send.at[k, other],
                recv_sem=near_recv.at[k, other],
                device_id={"dp": dp, "blk": lax.rem(blk + other, nblk)},
                device_id_type=MESH,
            )
            relay.start()
            relays.append(relay)
    for copy in away:
        copy.wait_send()
    for relay in relays:
        relay.wait()


def finish_kernel(codes_ref, weights_ref, vectors_ref, books_ref, book_out, residual_out, sum_out, parts):
    step = pl.program_id(0)
    rows, width = vectors_ref.shape
    ncg = books_ref.shape[0]

    @pl.when(step == 0)
    def _():
        sum_out[...] = jnp.zeros_like(sum_out)
        for q in range(M):
            book = jnp.concatenate([books_ref[c, q] for c in range(ncg)], axis=0).T
            book_out[q] = book
            high, low = split2(book)
            parts[q, :, :width] = high
            parts[q, :, width:] = low

    levels = lax.broadcasted_iota(jnp.int32, (rows, K), 1)
    codes = codes_ref[...]
    total = jnp.zeros((rows, 2 * width), F32)
    for q in range(M):
        hot = jnp.where(levels == codes[:, q : q + 1], 1.0, 0.0).astype(BF16)
        total = total + jnp.dot(hot, parts[q], preferred_element_type=F32)
    residual = vectors_ref[...] - (total[:, :width] + total[:, width:])
    residual_out[...] = residual
    weighted = weights_ref[...] * residual * residual
    sum_out[...] += jnp.broadcast_to(jnp.sum(weighted, keepdims=True), sum_out.shape)


def total_kernel(n, width, part_ref, count_ref, out_ref, gathered, send_sem, recv_sem):
    me = lax.axis_index("dp")
    barrier = pltpu.get_barrier_semaphore()

    def greet(k, carry):
        pl.semaphore_signal(barrier, inc=1, device_id={"dp": lax.rem(me + k, n)}, device_id_type=MESH)
        return carry

    lax.fori_loop(1, n, greet, 0)
    mass = jnp.sum(count_ref[0, 0:1, :]) * width
    pl.semaphore_wait(barrier, n - 1)

    def copy(k):
        return pltpu.make_async_remote_copy(
            src_ref=part_ref,
            dst_ref=gathered.at[me],
            send_sem=send_sem.at[k],
            recv_sem=recv_sem.at[k],
            device_id={"dp": lax.rem(me + k, n)},
            device_id_type=MESH,
        )

    def start(k, carry):
        copy(k).start()
        return carry

    def finish(k, carry):
        copy(k).wait()
        return carry

    lax.fori_loop(1, n, start, 0)
    gathered[me] = part_ref[...]
    lax.fori_loop(1, n, finish, 0)

    def add(s, total):
        return total + gathered[s]

    out_ref[...] = lax.fori_loop(1, n, add, gathered[0]) / mass


def body(vectors, codes, weights, ridge):
    rows, width = vectors.shape
    n, nblk = lax.axis_size("dp"), lax.axis_size("blk")
    gsz = M // nblk
    ncg = column_groups(n // gsz, width)
    cols = width // ncg
    mass = weights.astype(F32)
    codes_t = codes.T
    mass_row = mass[None, :]
    shape = jax.ShapeDtypeStruct

    part = pl.pallas_call(
        functools.partial(partial_kernel, ncg, nblk),
        out_shape=shape((ncg, gsz, cols, K), F32),
        in_specs=[vmem()] * 3,
        out_specs=vmem(),
        name="partial",
    )(codes_t, mass_row, vectors)

    all_codes, all_mass, pieces = pl.pallas_call(
        functools.partial(exchange_kernel, n, ncg, gsz),
        out_shape=(shape((n, M, rows), jnp.int32), shape((n, 1, rows), F32), shape((n, cols, K), F32)),
        in_specs=[vmem()] * 3,
        out_specs=(anywhere(),) * 3,
        scratch_shapes=[
            pltpu.SemaphoreType.DMA((3, n)),
            pltpu.SemaphoreType.DMA((3, n)),
            pltpu.SemaphoreType.DMA((3,)),
        ],
        compiler_params=pltpu.CompilerParams(collective_id=0, has_side_effects=True),
        name="exchange",
    )(codes_t, mass_row, part)

    gram, counts = pl.pallas_call(
        functools.partial(gram_kernel, nblk, gsz),
        grid=(n,),
        out_shape=(shape((M * K, 2 * K), BF16), shape((M, 8, K), F32)),
        in_specs=[
            pl.BlockSpec((1, M, rows), lambda i: (i, 0, 0)),
            pl.BlockSpec((1, 1, rows), lambda i: (i, 0, 0)),
        ],
        out_specs=(
            pl.BlockSpec((M * K, 2 * K), lambda i: (0, 0)),
            pl.BlockSpec((M, 8, K), lambda i: (0, 0, 0)),
        ),
        scratch_shapes=[pltpu.VMEM((M * K, K), F32)],
        compiler_params=pltpu.CompilerParams(dimension_semantics=("arbitrary",)),
        name="gram",
    )(all_codes, all_mass)

    state = pltpu.VMEM((M, cols, K), F32)
    dma = pltpu.SemaphoreType.DMA
    books = pl.pallas_call(
        functools.partial(solve_kernel, n, nblk, ncg, gsz),
        out_shape=shape((ncg, M, cols, K), F32),
        in_specs=[pl.BlockSpec(memory_space=pltpu.SMEM)] + [vmem()] * 3,
        out_specs=vmem(),
        scratch_shapes=[
            pltpu.VMEM((2, M, cols, K), F32), state, state, state, pltpu.VMEM((M, 8, K), F32),
            dma((2, M)), dma((2, M)), dma((ncg,)), dma((ncg,)), dma((ncg, nblk)), dma((ncg, nblk)),
        ],
        compiler_params=pltpu.CompilerParams(collective_id=1, has_side_effects=True),
        name="solve",
    )(ridge, gram, counts, pieces)

    step_rows = min(256, rows)
    codebooks, residual, local = pl.pallas_call(
        finish_kernel,
        grid=(rows // step_rows,),
        out_shape=(shape((M, K, width), F32), shape((rows, width), F32), shape((8, 128), F32)),
        in_specs=[
            pl.BlockSpec((step_rows, M), lambda i: (i, 0)),
            pl.BlockSpec((step_rows, 1), lambda i: (i, 0)),
            pl.BlockSpec((step_rows, width), lambda i: (i, 0)),
            pl.BlockSpec((ncg, M, cols, K), lambda i: (0, 0, 0, 0)),
        ],
        out_specs=(
            pl.BlockSpec((M, K, width), lambda i: (0, 0, 0)),
            pl.BlockSpec((step_rows, width), lambda i: (i, 0)),
            pl.BlockSpec((8, 128), lambda i: (0, 0)),
        ),
        scratch_shapes=[pltpu.VMEM((M, K, 2 * width), BF16)],
        compiler_params=pltpu.CompilerParams(dimension_semantics=("arbitrary",)),
        name="finish",
    )(codes, mass[:, None], vectors, books)

    distortion = pl.pallas_call(
        functools.partial(total_kernel, n, width),
        out_shape=shape((8, 128), F32),
        in_specs=[vmem()] * 2,
        out_specs=vmem(),
        scratch_shapes=[pltpu.VMEM((n, 8, 128), F32), dma((n,)), dma((n,))],
        compiler_params=pltpu.CompilerParams(collective_id=2, has_side_effects=True),
        name="total",
    )(local, counts)
    return (codebooks, residual, distortion[0, 0])


def solution(mesh):
    return jax.shard_map(
        body,
        mesh=mesh,
        in_specs=(P("dp", None), P("dp", None), P("dp"), P()),
        out_specs=(P(), P("dp", None), P()),
        check_vma=False,
    )
```

```python
import functools

import jax
import jax.numpy as jnp
from jax import lax
from jax.experimental import pallas as pl
from jax.experimental.pallas import tpu as pltpu
from jax.sharding import PartitionSpec as P

K = 256
M = 8
ITERS = 8
MESH = pl.DeviceIdType.MESH
HIGH = lax.Precision.HIGHEST
F32 = jnp.float32
BF16 = jnp.bfloat16
NT = (((1,), (1,)), ((), ()))


def vmem():
    return pl.BlockSpec(memory_space=pltpu.VMEM)


def split2(value):
    high = value.astype(BF16)
    low = (value - high.astype(F32)).astype(BF16)
    return high, low


def split3(value):
    high = value.astype(BF16)
    rest = value - high.astype(F32)
    middle = rest.astype(BF16)
    low = (rest - middle.astype(F32)).astype(BF16)
    return high, middle, low


def column_groups(groups, width):
    best = 1
    for count in range(1, groups + 1):
        if groups % count == 0 and width % count == 0 and (width // count) % 8 == 0:
            best = count
    return best


def hot_t(row, levels):
    return jnp.where(levels == row, jnp.ones((), BF16), jnp.zeros((), BF16))


def flip(value, mask, size):
    total, digit = 0, 1
    while digit < size:
        total = total + digit * lax.rem(value // digit + mask // digit % 2, 2)
        digit *= 2
    return total


def column(pieces):
    total = pieces[0]
    for piece in pieces[1:]:
        total = total + piece
    return jnp.sum(total, axis=1, keepdims=True)


def kernel(n, nblk, ncg, ridge_ref, codes_ref, mass_ref, vectors_ref, book_out, residual_out, sum_out,
           codes_all, mass_all, part, pieces, gram, halves, swap, solution, remain, direction, inverse,
           books, parts, gathered, send_sem, recv_sem, swap_send, swap_recv, far_send, far_recv,
           near_send, near_recv, sum_send, sum_recv):
    width, rows = vectors_ref.shape
    gsz = M // nblk
    cols = width // ncg
    me = lax.axis_index("dp")
    blk = lax.axis_index("blk")
    group, member = me // gsz, lax.rem(me, gsz)
    book = nblk * member + blk
    mine = lax.rem(group, ncg)
    bases = group - mine
    half = M // nblk
    peers = [(dm, db) for dm in range(gsz - 1, -1, -1) for db in range(nblk - 1, -1, -1) if (dm, db) != (0, 0)]

    def chip(k):
        return {"dp": lax.rem(me + k, n)}

    def team(dm, db):
        return {"dp": group * gsz + flip(member, dm, gsz), "blk": lax.rem(blk + db, nblk)}

    def far(k):
        return {"dp": (bases + lax.rem(mine + k, ncg)) * gsz + member, "blk": blk}

    def remote(source, target, send, recv, to):
        return pltpu.make_async_remote_copy(
            src_ref=source, dst_ref=target, send_sem=send, recv_sem=recv, device_id=to, device_id_type=MESH
        )

    def loop(function):
        def step(k, carry):
            function(k)
            return carry

        lax.fori_loop(1, n, step, 0)

    barrier = pltpu.get_barrier_semaphore()
    loop(lambda k: pl.semaphore_signal(barrier, inc=1, device_id=chip(k), device_id_type=MESH))
    others = [(dm, db) for dm, db in peers if db]
    for dm, db in others:
        pl.semaphore_signal(barrier, inc=1, device_id=team(dm, db), device_id_type=MESH)

    triple = jnp.concatenate(split3(vectors_ref[...]), axis=0)
    levels = lax.broadcasted_iota(jnp.int32, (K, rows), 0).astype(F32).astype(BF16)

    def spread(row, mass):
        return jnp.where(levels == row.astype(F32).astype(BF16), jnp.broadcast_to(mass, (K, rows)), jnp.zeros((), BF16))

    for m in range(gsz):
        hot = spread(codes_ref[pl.ds(nblk * m + blk, 1), :], mass_ref[...].astype(BF16))
        sums = lax.dot_general(triple, hot, NT, preferred_element_type=F32)
        total = sums[:width] + sums[width : 2 * width] + sums[2 * width :]
        for c in range(ncg):
            part[c, m] = total[c * cols : (c + 1) * cols]
    pl.semaphore_wait(barrier, n - 1 + len(others))

    def codes_copy(k):
        return remote(codes_ref, codes_all.at[me], send_sem.at[0, k], recv_sem.at[0, k], chip(k))

    def mass_copy(k):
        return remote(mass_ref, mass_all.at[me], send_sem.at[1, k], recv_sem.at[1, k], chip(k))

    def piece_copy(k):
        to = lax.rem(me + k, n)
        piece = part.at[lax.rem(to // gsz, ncg), lax.rem(to, gsz)]
        return remote(piece, pieces.at[me], send_sem.at[2, k], recv_sem.at[2, k], chip(k))

    def send_codes(k):
        codes_copy(k).start()
        mass_copy(k).start()

    loop(send_codes)
    loop(lambda k: piece_copy(k).start())

    codes_all[me] = codes_ref[...]
    mass_all[me] = mass_ref[...]
    pieces[me] = part[mine, member]
    gram[...] = jnp.zeros_like(gram)

    def block(q):
        return pl.ds(pl.multiple_of(q * K, K), K)

    def accumulate(source):
        weighted = spread(codes_all[source, pl.ds(book, 1), :], mass_all[source].astype(BF16))
        for j in range(1, M):
            other = lax.rem(book + j, M)
            hot = spread(codes_all[source, pl.ds(other, 1), :], jnp.ones((1, 1), BF16))
            gram[block(other), :] += lax.dot_general(hot, weighted, NT, preferred_element_type=F32)

    accumulate(me)

    def arrive(k):
        codes_copy(k).wait_recv()
        mass_copy(k).wait_recv()
        accumulate(lax.rem(me - k + n, n))

    loop(arrive)

    square = (K, K)
    own = jnp.sum(gram[block(lax.rem(book + 1, M)), :], axis=0, keepdims=True)
    diagonal = lax.broadcasted_iota(jnp.int32, square, 0) == lax.broadcasted_iota(jnp.int32, square, 1)
    gram[block(book), :] = jnp.where(diagonal, jnp.broadcast_to(own, square), 0.0)
    ones = jnp.ones((8, K), F32)
    for q in range(M):
        value = gram[block(q), :]
        high, low = split2(value)
        halves[block(q), :K] = high
        halves[block(q), K:] = low
        inverse[q] = lax.dot_general(ones, value, NT, precision=HIGH, preferred_element_type=F32)
    whole = jnp.sum(inverse[0, 0:1, :])
    lam = ridge_ref[0] * (whole / K)
    for q in range(M):
        inverse[q] = 1.0 / (inverse[q] + lam)

    loop(lambda k: piece_copy(k).wait_recv())
    right = lax.fori_loop(1, n, lambda s, total: total + pieces[s], pieces[0])

    def share(slot, value):
        swap[slot, book] = value
        here = swap.at[slot, book]
        copies = [
            remote(here, here, swap_send.at[slot, i], swap_recv.at[slot, i], team(dm, db))
            for i, (dm, db) in enumerate(peers)
        ]
        for copy in copies:
            copy.start()
        for copy in copies:
            copy.wait()

    share(0, right)
    terms = []
    for q in range(M):
        r = swap[0, q]
        z = r * inverse[q, 0:1, :]
        remain[q] = r
        direction[q] = z
        solution[q] = jnp.zeros_like(r)
        terms.append(r * z)

    def iterate(step, inner):
        slot = lax.rem(step + 1, 2)
        product = None
        for q in range(M):
            left = jnp.concatenate(split2(direction[q]), axis=0)
            term = jnp.dot(left, halves[pl.ds(q * K, K), :], preferred_element_type=F32)
            product = term if product is None else product + term
        image = (product[:cols, :K] + product[cols:, :K]) + (product[:cols, K:] + product[cols:, K:])
        share(slot, image)
        terms = []
        for q in range(M):
            d = direction[q]
            terms.append(d * (swap[slot, q] + lam * d))
        alpha = inner / column(terms)
        terms = []
        for q in range(M):
            d = direction[q]
            r = remain[q] - alpha * (swap[slot, q] + lam * d)
            solution[q] = solution[q] + alpha * d
            remain[q] = r
            terms.append(r * (r * inverse[q, 0:1, :]))
        fresh = column(terms)
        beta = fresh / inner
        for q in range(M):
            direction[q] = remain[q] * inverse[q, 0:1, :] + beta * direction[q]
        return fresh

    lax.fori_loop(0, ITERS, iterate, column(terms))

    span = pl.ds(blk * half, half)
    away = [
        remote(solution.at[span], books.at[mine, span], far_send.at[k], far_recv.at[k], far(k)) for k in range(1, ncg)
    ]
    for copy in away:
        copy.start()
    for q in range(M):
        books[mine, q] = solution[q]
    relays = []
    for k in range(1, ncg):
        away[k - 1].wait_recv()
        there = books.at[lax.rem(mine - k + ncg, ncg), span]
        for db in range(1, nblk):
            relay = remote(there, there, near_send.at[k, db], near_recv.at[k, db], team(0, db))
            relay.start()
            relays.append(relay)
    for relay in relays:
        relay.wait()

    for q in range(M):
        value = jnp.concatenate([books[c, q] for c in range(ncg)], axis=0)
        book_out[q] = value
        high, low = split2(value)
        parts[q, :width, :] = high
        parts[q, width:, :] = low

    size = min(256, rows)
    short = lax.broadcasted_iota(jnp.int32, (K, size), 0).astype(F32).astype(BF16)

    def rebuild(turn, total):
        at = pl.ds(pl.multiple_of(turn * size, size), size)
        value = jnp.zeros((2 * width, size), F32)
        for q in range(M):
            row = codes_ref[q : q + 1, at].astype(F32).astype(BF16)
            value = value + jnp.dot(parts[q], hot_t(row, short), preferred_element_type=F32)
        residual = vectors_ref[:, at] - (value[:width] + value[width:])
        residual_out[:, at] = residual
        return total + mass_ref[:, at] * (residual * residual)

    total = lax.fori_loop(0, rows // size, rebuild, jnp.zeros((width, size), F32))
    gathered[me] = jnp.broadcast_to(jnp.sum(total, keepdims=True), (8, 128))

    def sum_copy(k):
        return remote(gathered.at[me], gathered.at[me], sum_send.at[k], sum_recv.at[k], chip(k))

    loop(lambda k: sum_copy(k).start())
    for copy in away:
        copy.wait_send()

    def drain(k):
        codes_copy(k).wait_send()
        mass_copy(k).wait_send()
        piece_copy(k).wait_send()

    loop(drain)
    loop(lambda k: sum_copy(k).wait())
    final = lax.fori_loop(1, n, lambda s, value: value + gathered[s], gathered[0])
    sum_out[...] = final / (whole * width)


def body(vectors, codes, weights, ridge):
    rows, width = vectors.shape
    n, nblk = lax.axis_size("dp"), lax.axis_size("blk")
    gsz = M // nblk
    ncg = column_groups(n // gsz, width)
    cols = width // ncg
    shape = jax.ShapeDtypeStruct
    dma = pltpu.SemaphoreType.DMA
    state = pltpu.VMEM((M, cols, K), F32)
    books, residual, distortion = pl.pallas_call(
        functools.partial(kernel, n, nblk, ncg),
        out_shape=(shape((M, width, K), F32), shape((width, rows), F32), shape((8, 128), F32)),
        in_specs=[pl.BlockSpec(memory_space=pltpu.SMEM)] + [vmem()] * 3,
        out_specs=(vmem(),) * 3,
        scratch_shapes=[
            pltpu.VMEM((n, M, rows), jnp.int32),
            pltpu.VMEM((n, 1, rows), F32),
            pltpu.VMEM((ncg, gsz, cols, K), F32),
            pltpu.VMEM((n, cols, K), F32),
            pltpu.VMEM((M * K, K), F32),
            pltpu.VMEM((M * K, 2 * K), BF16),
            pltpu.VMEM((2, M, cols, K), F32),
            state,
            state,
            state,
            pltpu.VMEM((M, 8, K), F32),
            pltpu.VMEM((ncg, M, cols, K), F32),
            pltpu.VMEM((M, 2 * width, K), BF16),
            pltpu.VMEM((n, 8, 128), F32),
            dma((3, n)),
            dma((3, n)),
            dma((2, M)),
            dma((2, M)),
            dma((ncg,)),
            dma((ncg,)),
            dma((ncg, nblk)),
            dma((ncg, nblk)),
            dma((n,)),
            dma((n,)),
        ],
        compiler_params=pltpu.CompilerParams(collective_id=0, has_side_effects=True),
        name="update",
    )(ridge, codes.T, weights.astype(F32)[None, :], vectors.T)
    return (books.transpose(0, 2, 1), residual.T, distortion[0, 0])


def solution(mesh):
    return jax.shard_map(
        body,
        mesh=mesh,
        in_specs=(P("dp", None), P("dp", None), P("dp"), P()),
        out_specs=(P(), P("dp", None), P()),
        check_vma=False,
    )
```

```python
import functools

import jax
import jax.numpy as jnp
from jax import lax
from jax.experimental import pallas as pl
from jax.experimental.pallas import tpu as pltpu
from jax.sharding import PartitionSpec as P

K = 256
M = 8
ITERS = 8
MESH = pl.DeviceIdType.MESH
HIGH = lax.Precision.HIGHEST
F32 = jnp.float32
BF16 = jnp.bfloat16
NT = (((1,), (1,)), ((), ()))


def vmem():
    return pl.BlockSpec(memory_space=pltpu.VMEM)


def split2(value):
    high = value.astype(BF16)
    low = (value - high.astype(F32)).astype(BF16)
    return high, low


def split3(value):
    high = value.astype(BF16)
    rest = value - high.astype(F32)
    middle = rest.astype(BF16)
    low = (rest - middle.astype(F32)).astype(BF16)
    return high, middle, low


def column_groups(groups, width):
    best = 1
    for count in range(1, groups + 1):
        if groups % count == 0 and width % count == 0 and (width // count) % 8 == 0:
            best = count
    return best


def hot_t(row, levels):
    return jnp.where(levels == row, jnp.ones((), BF16), jnp.zeros((), BF16))


def flip(value, mask, size):
    total, digit = 0, 1
    while digit < size:
        total = total + digit * lax.rem(value // digit + mask // digit % 2, 2)
        digit *= 2
    return total


def column(pieces):
    total = pieces[0]
    for piece in pieces[1:]:
        total = total + piece
    return jnp.sum(total, axis=1, keepdims=True)


def kernel(n, nblk, ncg, ridge_ref, codes_ref, mass_ref, vectors_ref, book_out, residual_out, sum_out,
           codes_all, mass_all, part, pieces, gram, halves, swap, solution, remain, direction, inverse,
           books, parts, gathered, send_sem, recv_sem, swap_send, swap_recv, far_send, far_recv,
           near_send, near_recv, sum_send, sum_recv):
    width, rows = vectors_ref.shape
    gsz = M // nblk
    cols = width // ncg
    me = lax.axis_index("dp")
    blk = lax.axis_index("blk")
    group, member = me // gsz, lax.rem(me, gsz)
    book = nblk * member + blk
    mine = lax.rem(group, ncg)
    bases = group - mine
    half = M // nblk
    peers = [(dm, db) for dm in range(gsz - 1, -1, -1) for db in range(nblk - 1, -1, -1) if (dm, db) != (0, 0)]

    def chip(k):
        return {"dp": lax.rem(me + k, n)}

    def team(dm, db):
        return {"dp": group * gsz + flip(member, dm, gsz), "blk": lax.rem(blk + db, nblk)}

    def far(k):
        return {"dp": (bases + lax.rem(mine + k, ncg)) * gsz + member, "blk": blk}

    def remote(source, target, send, recv, to):
        return pltpu.make_async_remote_copy(
            src_ref=source, dst_ref=target, send_sem=send, recv_sem=recv, device_id=to, device_id_type=MESH
        )

    def loop(function):
        def step(k, carry):
            function(k)
            return carry

        lax.fori_loop(1, n, step, 0)

    barrier = pltpu.get_barrier_semaphore()
    loop(lambda k: pl.semaphore_signal(barrier, inc=1, device_id=chip(k), device_id_type=MESH))
    others = [(dm, db) for dm, db in peers if db]
    for dm, db in others:
        pl.semaphore_signal(barrier, inc=1, device_id=team(dm, db), device_id_type=MESH)

    triple = jnp.concatenate(split3(vectors_ref[...]), axis=0)
    levels = lax.broadcasted_iota(jnp.int32, (K, rows), 0).astype(F32).astype(BF16)

    def spread(row, mass):
        return jnp.where(levels == row.astype(F32).astype(BF16), jnp.broadcast_to(mass, (K, rows)), jnp.zeros((), BF16))

    for m in range(gsz):
        hot = spread(codes_ref[pl.ds(nblk * m + blk, 1), :], mass_ref[...].astype(BF16))
        sums = lax.dot_general(triple, hot, NT, preferred_element_type=F32)
        total = sums[:width] + sums[width : 2 * width] + sums[2 * width :]
        for c in range(ncg):
            part[c, m] = total[c * cols : (c + 1) * cols]
    pl.semaphore_wait(barrier, n - 1 + len(others))

    def codes_copy(k):
        return remote(codes_ref, codes_all.at[me], send_sem.at[0, k], recv_sem.at[0, k], chip(k))

    def mass_copy(k):
        return remote(mass_ref, mass_all.at[me], send_sem.at[1, k], recv_sem.at[1, k], chip(k))

    def piece_copy(k):
        to = lax.rem(me + k, n)
        piece = part.at[lax.rem(to // gsz, ncg), lax.rem(to, gsz)]
        return remote(piece, pieces.at[me], send_sem.at[2, k], recv_sem.at[2, k], chip(k))

    def send_codes(k):
        codes_copy(k).start()
        mass_copy(k).start()

    loop(send_codes)

    codes_all[me] = codes_ref[...]
    mass_all[me] = mass_ref[...]
    pieces[me] = part[mine, member]
    gram[...] = jnp.zeros_like(gram)

    def block(q):
        return pl.ds(pl.multiple_of(q * K, K), K)

    def accumulate(source):
        weighted = spread(codes_all[source, pl.ds(book, 1), :], mass_all[source].astype(BF16))
        for j in range(1, M):
            other = lax.rem(book + j, M)
            hot = spread(codes_all[source, pl.ds(other, 1), :], jnp.ones((1, 1), BF16))
            gram[block(other), :] += lax.dot_general(hot, weighted, NT, preferred_element_type=F32)

    accumulate(me)

    def arrive(k):
        codes_copy(k).wait_recv()
        mass_copy(k).wait_recv()
        piece_copy(k).start()
        accumulate(lax.rem(me - k + n, n))

    loop(arrive)

    square = (K, K)
    own = jnp.sum(gram[block(lax.rem(book + 1, M)), :], axis=0, keepdims=True)
    diagonal = lax.broadcasted_iota(jnp.int32, square, 0) == lax.broadcasted_iota(jnp.int32, square, 1)
    gram[block(book), :] = jnp.where(diagonal, jnp.broadcast_to(own, square), 0.0)
    ones = jnp.ones((8, K), F32)
    for q in range(M):
        value = gram[block(q), :]
        high, low = split2(value)
        halves[block(q), :K] = high
        halves[block(q), K:] = low
        inverse[q] = lax.dot_general(ones, value, NT, precision=HIGH, preferred_element_type=F32)
    whole = jnp.sum(inverse[0, 0:1, :])
    lam = ridge_ref[0] * (whole / K)
    for q in range(M):
        inverse[q] = 1.0 / (inverse[q] + lam)

    loop(lambda k: piece_copy(k).wait_recv())
    right = lax.fori_loop(1, n, lambda s, total: total + pieces[s], pieces[0])

    cut = (cols // 8 + 1) // 2 * 8
    streams = [(i, pl.ds(first, last - first), last - first) for i, (first, last) in enumerate([(0, cut), (cut, cols)]) if last > first]

    def copies(stream, slot):
        i, span, _ = stream
        here = swap.at[slot, book, span]
        return [
            remote(here, here, swap_send.at[slot, i, j], swap_recv.at[slot, i, j], team(dm, db))
            for j, (dm, db) in enumerate(peers)
        ]

    def send(stream, slot, value):
        swap[slot, book, stream[1]] = value
        for copy in copies(stream, slot):
            copy.start()

    def receive(stream, slot):
        for copy in copies(stream, slot):
            copy.wait()

    def apply(stream):
        _, span, size = stream
        product = None
        for q in range(M):
            left = jnp.concatenate(split2(direction[q, span]), axis=0)
            term = jnp.dot(left, halves[pl.ds(q * K, K), :], preferred_element_type=F32)
            product = term if product is None else product + term
        return (product[:size, :K] + product[size:, :K]) + (product[:size, K:] + product[size:, K:])

    def begin(stream):
        _, span, _ = stream
        receive(stream, 0)
        terms = []
        for q in range(M):
            r = swap[0, q, span]
            z = r * inverse[q, 0:1, :]
            remain[q, span] = r
            direction[q, span] = z
            solution[q, span] = jnp.zeros_like(r)
            terms.append(r * z)
        send(stream, 1, apply(stream))
        return column(terms)

    def advance(stream, slot, inner):
        _, span, _ = stream
        receive(stream, slot)
        terms = []
        for q in range(M):
            d = direction[q, span]
            terms.append(d * (swap[slot, q, span] + lam * d))
        alpha = inner / column(terms)
        terms = []
        for q in range(M):
            d = direction[q, span]
            r = remain[q, span] - alpha * (swap[slot, q, span] + lam * d)
            solution[q, span] = solution[q, span] + alpha * d
            remain[q, span] = r
            terms.append(r * (r * inverse[q, 0:1, :]))
        fresh = column(terms)
        beta = fresh / inner
        for q in range(M):
            direction[q, span] = remain[q, span] * inverse[q, 0:1, :] + beta * direction[q, span]
        return fresh

    def iterate(step, inners):
        slot = lax.rem(step, 2)
        results = []
        for stream, inner in zip(streams, inners):
            results.append(advance(stream, slot, inner))
            send(stream, 1 - slot, apply(stream))
        return tuple(results)

    for stream in streams:
        first = stream[1].start
        send(stream, 0, right[first : first + stream[2]])
    inners = lax.fori_loop(1, ITERS, iterate, tuple(begin(stream) for stream in streams))
    for stream, inner in zip(streams, inners):
        advance(stream, ITERS % 2, inner)

    span = pl.ds(blk * half, half)
    away = [
        remote(solution.at[span], books.at[mine, span], far_send.at[k], far_recv.at[k], far(k)) for k in range(1, ncg)
    ]
    for copy in away:
        copy.start()
    for q in range(M):
        books[mine, q] = solution[q]
    relays = []
    for k in range(1, ncg):
        away[k - 1].wait_recv()
        there = books.at[lax.rem(mine - k + ncg, ncg), span]
        for db in range(1, nblk):
            relay = remote(there, there, near_send.at[k, db], near_recv.at[k, db], team(0, db))
            relay.start()
            relays.append(relay)
    for relay in relays:
        relay.wait()

    for q in range(M):
        value = jnp.concatenate([books[c, q] for c in range(ncg)], axis=0)
        book_out[q] = value
        high, low = split2(value)
        parts[q, :width, :] = high
        parts[q, width:, :] = low

    size = min(256, rows)
    short = lax.broadcasted_iota(jnp.int32, (K, size), 0).astype(F32).astype(BF16)

    def rebuild(turn, total):
        at = pl.ds(pl.multiple_of(turn * size, size), size)
        value = jnp.zeros((2 * width, size), F32)
        for q in range(M):
            row = codes_ref[q : q + 1, at].astype(F32).astype(BF16)
            value = value + jnp.dot(parts[q], hot_t(row, short), preferred_element_type=F32)
        residual = vectors_ref[:, at] - (value[:width] + value[width:])
        residual_out[:, at] = residual
        return total + mass_ref[:, at] * (residual * residual)

    total = lax.fori_loop(0, rows // size, rebuild, jnp.zeros((width, size), F32))
    gathered[me] = jnp.broadcast_to(jnp.sum(total, keepdims=True), (8, 128))

    def sum_copy(k):
        return remote(gathered.at[me], gathered.at[me], sum_send.at[k], sum_recv.at[k], chip(k))

    loop(lambda k: sum_copy(k).start())
    for copy in away:
        copy.wait_send()

    def drain(k):
        codes_copy(k).wait_send()
        mass_copy(k).wait_send()
        piece_copy(k).wait_send()

    loop(drain)
    loop(lambda k: sum_copy(k).wait())
    final = lax.fori_loop(1, n, lambda s, value: value + gathered[s], gathered[0])
    sum_out[...] = final / (whole * width)


def body(vectors, codes, weights, ridge):
    rows, width = vectors.shape
    n, nblk = lax.axis_size("dp"), lax.axis_size("blk")
    gsz = M // nblk
    ncg = column_groups(n // gsz, width)
    cols = width // ncg
    shape = jax.ShapeDtypeStruct
    dma = pltpu.SemaphoreType.DMA
    state = pltpu.VMEM((M, cols, K), F32)
    books, residual, distortion = pl.pallas_call(
        functools.partial(kernel, n, nblk, ncg),
        out_shape=(shape((M, width, K), F32), shape((width, rows), F32), shape((8, 128), F32)),
        in_specs=[pl.BlockSpec(memory_space=pltpu.SMEM)] + [vmem()] * 3,
        out_specs=(vmem(),) * 3,
        scratch_shapes=[
            pltpu.VMEM((n, M, rows), jnp.int32),
            pltpu.VMEM((n, 1, rows), F32),
            pltpu.VMEM((ncg, gsz, cols, K), F32),
            pltpu.VMEM((n, cols, K), F32),
            pltpu.VMEM((M * K, K), F32),
            pltpu.VMEM((M * K, 2 * K), BF16),
            pltpu.VMEM((2, M, cols, K), F32),
            state,
            state,
            state,
            pltpu.VMEM((M, 8, K), F32),
            pltpu.VMEM((ncg, M, cols, K), F32),
            pltpu.VMEM((M, 2 * width, K), BF16),
            pltpu.VMEM((n, 8, 128), F32),
            dma((3, n)),
            dma((3, n)),
            dma((2, 2, M)),
            dma((2, 2, M)),
            dma((ncg,)),
            dma((ncg,)),
            dma((ncg, nblk)),
            dma((ncg, nblk)),
            dma((n,)),
            dma((n,)),
        ],
        compiler_params=pltpu.CompilerParams(collective_id=0, has_side_effects=True),
        name="update",
    )(ridge, codes.T, weights.astype(F32)[None, :], vectors.T)
    return (books.transpose(0, 2, 1), residual.T, distortion[0, 0])


def solution(mesh):
    return jax.shard_map(
        body,
        mesh=mesh,
        in_specs=(P("dp", None), P("dp", None), P("dp"), P()),
        out_specs=(P(), P("dp", None), P()),
        check_vma=False,
    )
```

```python
import functools

import jax
import jax.numpy as jnp
from jax import lax
from jax.experimental import pallas as pl
from jax.experimental.pallas import tpu as pltpu
from jax.sharding import PartitionSpec as P

K = 256
M = 8
ITERS = 8
MESH = pl.DeviceIdType.MESH
HIGH = lax.Precision.HIGHEST
F32 = jnp.float32
BF16 = jnp.bfloat16
NT = (((1,), (1,)), ((), ()))


def vmem():
    return pl.BlockSpec(memory_space=pltpu.VMEM)


def split2(value):
    high = value.astype(BF16)
    low = (value - high.astype(F32)).astype(BF16)
    return high, low


def split3(value):
    high = value.astype(BF16)
    rest = value - high.astype(F32)
    middle = rest.astype(BF16)
    low = (rest - middle.astype(F32)).astype(BF16)
    return high, middle, low


def column_groups(groups, width):
    best = 1
    for count in range(1, groups + 1):
        if groups % count == 0 and width % count == 0 and (width // count) % 8 == 0:
            best = count
    return best


def hot_t(row, levels):
    return jnp.where(levels == row, jnp.ones((), BF16), jnp.zeros((), BF16))


def flip(value, mask, size):
    total, digit = 0, 1
    while digit < size:
        total = total + digit * lax.rem(value // digit + mask // digit % 2, 2)
        digit *= 2
    return total


def column(pieces):
    total = pieces[0]
    for piece in pieces[1:]:
        total = total + piece
    return jnp.sum(total, axis=1, keepdims=True)


def kernel(n, nblk, ncg, ridge_ref, codes_ref, mass_ref, vectors_ref, book_out, residual_out, sum_out,
           codes_all, mass_all, part, pieces, gram, halves, swap, solution, remain, direction, inverse,
           books, parts, gathered, send_sem, recv_sem, swap_send, swap_recv, far_send, far_recv,
           near_send, near_recv, sum_send, sum_recv, pass_send, pass_recv):
    width, rows = vectors_ref.shape
    gsz = M // nblk
    cols = width // ncg
    me = lax.axis_index("dp")
    blk = lax.axis_index("blk")
    group, member = me // gsz, lax.rem(me, gsz)
    book = nblk * member + blk
    mine = lax.rem(group, ncg)
    bases = group - mine
    half = M // nblk
    peers = [(dm, db) for dm in range(gsz - 1, -1, -1) for db in range(nblk - 1, -1, -1) if (dm, db) != (0, 0)]

    def chip(k):
        return {"dp": lax.rem(me + k, n)}

    def team(dm, db):
        return {"dp": group * gsz + flip(member, dm, gsz), "blk": lax.rem(blk + db, nblk)}

    def far(k):
        return {"dp": (bases + lax.rem(mine + k, ncg)) * gsz + member, "blk": blk}

    def remote(source, target, send, recv, to):
        return pltpu.make_async_remote_copy(
            src_ref=source, dst_ref=target, send_sem=send, recv_sem=recv, device_id=to, device_id_type=MESH
        )

    def loop(function):
        def step(k, carry):
            function(k)
            return carry

        lax.fori_loop(1, n, step, 0)

    barrier = pltpu.get_barrier_semaphore()
    loop(lambda k: pl.semaphore_signal(barrier, inc=1, device_id=chip(k), device_id_type=MESH))
    others = [(dm, db) for dm, db in peers if db]
    for dm, db in others:
        pl.semaphore_signal(barrier, inc=1, device_id=team(dm, db), device_id_type=MESH)

    triple = jnp.concatenate(split3(vectors_ref[...]), axis=0)
    levels = lax.broadcasted_iota(jnp.int32, (K, rows), 0).astype(F32).astype(BF16)

    def spread(row, mass):
        return jnp.where(levels == row.astype(F32).astype(BF16), jnp.broadcast_to(mass, (K, rows)), jnp.zeros((), BF16))

    for m in range(gsz):
        hot = spread(codes_ref[pl.ds(nblk * m + blk, 1), :], mass_ref[...].astype(BF16))
        sums = lax.dot_general(triple, hot, NT, preferred_element_type=F32)
        total = sums[:width] + sums[width : 2 * width] + sums[2 * width :]
        for c in range(ncg):
            part[c, m] = total[c * cols : (c + 1) * cols]
    pl.semaphore_wait(barrier, n - 1 + len(others))

    share = rows // nblk
    lanes = pl.ds(pl.multiple_of(blk * share, share), share)

    def codes_copy(k):
        return remote(codes_ref.at[:, lanes], codes_all.at[me, :, lanes], send_sem.at[0, k], recv_sem.at[0, k], chip(k))

    def mass_copy(k):
        return remote(mass_ref.at[:, lanes], mass_all.at[me, :, lanes], send_sem.at[1, k], recv_sem.at[1, k], chip(k))

    def across(k):
        source = lax.rem(me - k + n, n)
        return [
            remote(ref.at[source, :, lanes], ref.at[source, :, lanes], pass_send.at[i, k, db], pass_recv.at[i, k, db], team(0, db))
            for i, ref in enumerate((codes_all, mass_all))
            for db in range(1, nblk)
        ]

    def piece_copy(k):
        to = lax.rem(me + k, n)
        piece = part.at[lax.rem(to // gsz, ncg), lax.rem(to, gsz)]
        return remote(piece, pieces.at[me], send_sem.at[2, k], recv_sem.at[2, k], chip(k))

    def send_codes(k):
        codes_copy(k).start()
        mass_copy(k).start()

    loop(send_codes)

    codes_all[me] = codes_ref[...]
    mass_all[me] = mass_ref[...]
    pieces[me] = part[mine, member]
    gram[...] = jnp.zeros_like(gram)

    def block(q):
        return pl.ds(pl.multiple_of(q * K, K), K)

    def accumulate(source):
        weighted = spread(codes_all[source, pl.ds(book, 1), :], mass_all[source].astype(BF16))
        for j in range(1, M):
            other = lax.rem(book + j, M)
            hot = spread(codes_all[source, pl.ds(other, 1), :], jnp.ones((1, 1), BF16))
            gram[block(other), :] += lax.dot_general(hot, weighted, NT, preferred_element_type=F32)

    def arrive(k):
        codes_copy(k).wait_recv()
        mass_copy(k).wait_recv()
        for copy in across(k):
            copy.start()
        piece_copy(k).start()

    def settle(k):
        for copy in across(k):
            copy.wait()
        accumulate(lax.rem(me - k + n, n))

    def turn(k, carry):
        arrive(k)
        settle(k - 1)
        return carry

    accumulate(me)
    arrive(1)
    lax.fori_loop(2, n, turn, 0)
    settle(n - 1)

    square = (K, K)
    own = jnp.sum(gram[block(lax.rem(book + 1, M)), :], axis=0, keepdims=True)
    diagonal = lax.broadcasted_iota(jnp.int32, square, 0) == lax.broadcasted_iota(jnp.int32, square, 1)
    gram[block(book), :] = jnp.where(diagonal, jnp.broadcast_to(own, square), 0.0)
    ones = jnp.ones((8, K), F32)
    for q in range(M):
        value = gram[block(q), :]
        high, low = split2(value)
        halves[block(q), :K] = high
        halves[block(q), K:] = low
        inverse[q] = lax.dot_general(ones, value, NT, precision=HIGH, preferred_element_type=F32)
    whole = jnp.sum(inverse[0, 0:1, :])
    lam = ridge_ref[0] * (whole / K)
    for q in range(M):
        inverse[q] = 1.0 / (inverse[q] + lam)

    loop(lambda k: piece_copy(k).wait_recv())
    right = lax.fori_loop(1, n, lambda s, total: total + pieces[s], pieces[0])

    cut = (cols // 8 + 1) // 2 * 8
    streams = [(i, pl.ds(first, last - first), last - first) for i, (first, last) in enumerate([(0, cut), (cut, cols)]) if last > first]

    def straight(stream, slot):
        i, span, _ = stream
        here = swap.at[slot, book, span]
        return {
            (dm, db): remote(here, here, swap_send.at[slot, i, j], swap_recv.at[slot, i, j], team(dm, db))
            for j, (dm, db) in enumerate(peers)
            if dm == 0 or db == 0
        }

    def send(stream, slot, value):
        swap[slot, book, stream[1]] = value
        for copy in straight(stream, slot).values():
            copy.start()

    def receive(stream, slot):
        i, span, _ = stream
        direct = straight(stream, slot)
        relays = []
        for dm in range(1, gsz):
            direct[dm, 0].wait_recv()
            there = swap.at[slot, nblk * flip(member, dm, gsz) + blk, span]
            for db in range(1, nblk):
                j = peers.index((dm, db))
                relay = remote(there, there, swap_send.at[slot, i, j], swap_recv.at[slot, i, j], team(0, db))
                relay.start()
                relays.append(relay)
        for db in range(1, nblk):
            direct[0, db].wait()
        for dm in range(1, gsz):
            direct[dm, 0].wait_send()
        for relay in relays:
            relay.wait()

    def apply(stream):
        _, span, size = stream
        product = None
        for q in range(M):
            left = jnp.concatenate(split2(direction[q, span]), axis=0)
            term = jnp.dot(left, halves[pl.ds(q * K, K), :], preferred_element_type=F32)
            product = term if product is None else product + term
        return (product[:size, :K] + product[size:, :K]) + (product[:size, K:] + product[size:, K:])

    def begin(stream):
        _, span, _ = stream
        receive(stream, 0)
        terms = []
        for q in range(M):
            r = swap[0, q, span]
            z = r * inverse[q, 0:1, :]
            remain[q, span] = r
            direction[q, span] = z
            solution[q, span] = jnp.zeros_like(r)
            terms.append(r * z)
        send(stream, 1, apply(stream))
        return column(terms)

    def advance(stream, slot, inner):
        _, span, _ = stream
        receive(stream, slot)
        terms = []
        for q in range(M):
            d = direction[q, span]
            terms.append(d * (swap[slot, q, span] + lam * d))
        alpha = inner / column(terms)
        terms = []
        for q in range(M):
            d = direction[q, span]
            r = remain[q, span] - alpha * (swap[slot, q, span] + lam * d)
            solution[q, span] = solution[q, span] + alpha * d
            remain[q, span] = r
            terms.append(r * (r * inverse[q, 0:1, :]))
        fresh = column(terms)
        beta = fresh / inner
        for q in range(M):
            direction[q, span] = remain[q, span] * inverse[q, 0:1, :] + beta * direction[q, span]
        return fresh

    def iterate(step, inners):
        slot = lax.rem(step, 2)
        results = []
        for stream, inner in zip(streams, inners):
            results.append(advance(stream, slot, inner))
            send(stream, 1 - slot, apply(stream))
        return tuple(results)

    for stream in streams:
        first = stream[1].start
        send(stream, 0, right[first : first + stream[2]])
    inners = lax.fori_loop(1, ITERS, iterate, tuple(begin(stream) for stream in streams))
    for stream, inner in zip(streams, inners):
        advance(stream, ITERS % 2, inner)

    span = pl.ds(blk * half, half)
    away = [
        remote(solution.at[span], books.at[mine, span], far_send.at[k], far_recv.at[k], far(k)) for k in range(1, ncg)
    ]
    for copy in away:
        copy.start()
    for q in range(M):
        books[mine, q] = solution[q]
    relays = []
    for k in range(1, ncg):
        away[k - 1].wait_recv()
        there = books.at[lax.rem(mine - k + ncg, ncg), span]
        for db in range(1, nblk):
            relay = remote(there, there, near_send.at[k, db], near_recv.at[k, db], team(0, db))
            relay.start()
            relays.append(relay)
    for relay in relays:
        relay.wait()

    for q in range(M):
        value = jnp.concatenate([books[c, q] for c in range(ncg)], axis=0)
        book_out[q] = value
        high, low = split2(value)
        parts[q, :width, :] = high
        parts[q, width:, :] = low

    size = min(256, rows)
    short = lax.broadcasted_iota(jnp.int32, (K, size), 0).astype(F32).astype(BF16)

    def rebuild(turn, total):
        at = pl.ds(pl.multiple_of(turn * size, size), size)
        value = jnp.zeros((2 * width, size), F32)
        for q in range(M):
            row = codes_ref[q : q + 1, at].astype(F32).astype(BF16)
            value = value + jnp.dot(parts[q], hot_t(row, short), preferred_element_type=F32)
        residual = vectors_ref[:, at] - (value[:width] + value[width:])
        residual_out[:, at] = residual
        return total + mass_ref[:, at] * (residual * residual)

    total = lax.fori_loop(0, rows // size, rebuild, jnp.zeros((width, size), F32))
    gathered[me] = jnp.broadcast_to(jnp.sum(total, keepdims=True), (8, 128))

    def sum_copy(k):
        return remote(gathered.at[me], gathered.at[me], sum_send.at[k], sum_recv.at[k], chip(k))

    loop(lambda k: sum_copy(k).start())
    for copy in away:
        copy.wait_send()

    def drain(k):
        codes_copy(k).wait_send()
        mass_copy(k).wait_send()
        piece_copy(k).wait_send()

    loop(drain)
    loop(lambda k: sum_copy(k).wait())
    final = lax.fori_loop(1, n, lambda s, value: value + gathered[s], gathered[0])
    sum_out[...] = final / (whole * width)


def body(vectors, codes, weights, ridge):
    rows, width = vectors.shape
    n, nblk = lax.axis_size("dp"), lax.axis_size("blk")
    gsz = M // nblk
    ncg = column_groups(n // gsz, width)
    cols = width // ncg
    shape = jax.ShapeDtypeStruct
    dma = pltpu.SemaphoreType.DMA
    state = pltpu.VMEM((M, cols, K), F32)
    books, residual, distortion = pl.pallas_call(
        functools.partial(kernel, n, nblk, ncg),
        out_shape=(shape((M, width, K), F32), shape((width, rows), F32), shape((8, 128), F32)),
        in_specs=[pl.BlockSpec(memory_space=pltpu.SMEM)] + [vmem()] * 3,
        out_specs=(vmem(),) * 3,
        scratch_shapes=[
            pltpu.VMEM((n, M, rows), jnp.int32),
            pltpu.VMEM((n, 1, rows), F32),
            pltpu.VMEM((ncg, gsz, cols, K), F32),
            pltpu.VMEM((n, cols, K), F32),
            pltpu.VMEM((M * K, K), F32),
            pltpu.VMEM((M * K, 2 * K), BF16),
            pltpu.VMEM((2, M, cols, K), F32),
            state,
            state,
            state,
            pltpu.VMEM((M, 8, K), F32),
            pltpu.VMEM((ncg, M, cols, K), F32),
            pltpu.VMEM((M, 2 * width, K), BF16),
            pltpu.VMEM((n, 8, 128), F32),
            dma((3, n)),
            dma((3, n)),
            dma((2, 2, M)),
            dma((2, 2, M)),
            dma((ncg,)),
            dma((ncg,)),
            dma((ncg, nblk)),
            dma((ncg, nblk)),
            dma((n,)),
            dma((n,)),
            dma((2, n, nblk)),
            dma((2, n, nblk)),
        ],
        compiler_params=pltpu.CompilerParams(collective_id=0, has_side_effects=True),
        name="update",
    )(ridge, codes.T, weights.astype(F32)[None, :], vectors.T)
    return (books.transpose(0, 2, 1), residual.T, distortion[0, 0])


def solution(mesh):
    return jax.shard_map(
        body,
        mesh=mesh,
        in_specs=(P("dp", None), P("dp", None), P("dp"), P()),
        out_specs=(P(), P("dp", None), P()),
        check_vma=False,
    )
```
